32 devices in a mesh: dp: 8 (over z, y), expert: 4 (over x, core).
Axes of the slice: x: 2, y: 2, z: 4, core: 2. Of those that a mesh axis runs over, the one named last changes fastest.
Arguments:
- tokens: bfloat16 [4096, 2048], P(('dp', 'expert')), may hold values from -6 to 6
- cotangent: bfloat16 [4096, 2048], P(('dp', 'expert')), may hold values from -6 to 6
- expert_ids: int32 [4096, 2], P(('dp', 'expert')), may hold values from 0 to 3, all different within a row; in each aligned block of 128 rows (0 to 127, 128 to 255, ...) at most 72 rows name the same one
- gate_values: bfloat16 [4096, 2], P(('dp', 'expert')), may hold values from 0.099609375 to 1
- gate_weights: bfloat16 [4, 2048, 512], P('expert'), may hold values from -0.125 to 0.125
- up_weights: bfloat16 [4, 2048, 512], P('expert'), may hold values from -0.125 to 0.125
- down_weights: bfloat16 [4, 512, 2048], P('expert'), may hold values from -0.25 to 0.25
Outputs:
- token_grads: bfloat16 [4096, 2048], P(('dp', 'expert'))
- down_grads: float32 [4, 512, 2048], P('expert', 'dp')
The draws below stay inside these ranges and needn't reach their ends.
Inputs may be any that keep to these rules, and one draw needn't show every extreme that they name: `expert_ids`: within the rows of one device, each expert is named by at most 72 slots, and by exactly 72 slots in the rows of some device.
All inputs are finite; a program needn't handle non-finite values.
Results may differ from the reference program's by a relative error of at most 0.0065.
Values may be sent and summed in bfloat16 or wider, within the bound.
No kernel may reach another device: no remote copies, remote signals or barrier semaphores. Data moves between devices by JAX's collectives and lax.ppermute only.
A program may use at most 64 MiB of HBM per device.

```python
import math
import jax
import jax.numpy as jnp
import numpy as np
from jax import lax

D = 2048
F = 512
TOP = 2
TOK_DEV = 128
EXPERTS = 4
CAP = 72
TOKENS = 4096


def steps_of(stream_key, dims, split, smallest, high):
    def one(axis_at, parts):
        draws = jax.random.uniform(jax.random.fold_in(jax.random.fold_in(stream_key, 6), axis_at), (parts,), jnp.float32, smallest / len(split), high / len(split))
        return jnp.repeat(jnp.exp(draws), dims[axis_at] // parts).reshape((-1,) + (1,) * (len(dims) - axis_at - 1))

    gain = one(*split[0])
    for cut in split[1:]:
        gain = gain * one(*cut)
    return gain


def assign_block(rng, own, number, rows, number_of, top, limit, skew):
    sequence = jax.random.permutation(rng, number_of)
    packed, usual = portions_of(number_of, rows * top, limit, skew, True), portions_of(number_of, rows * top, limit, skew, False)
    places = jnp.arange(number_of)

    def named(tallies, rotation):
        used = int((tallies > 0).sum())
        fixed = max(1, used // 4)
        shifted = fixed + (places - fixed + rotation * (used - fixed)) % max(1, number_of - fixed)
        return jnp.zeros((number_of,), jnp.int32).at[sequence[jnp.where(places < fixed, places, shifted)]].set(jnp.asarray(tallies, jnp.int32))

    tallies = jnp.where(number % 4 == 0, named(packed, number // 4), named(usual, number - number // 4 - 1))
    mixed = jax.random.permutation(jax.random.fold_in(own, 3), number_of)
    source_of, sink = mixed[0:number_of // 2 * 2:2], mixed[1:number_of // 2 * 2:2]
    room = jnp.minimum(tallies[source_of] - 1, limit - tallies[sink]) // 2
    room = jnp.where((source_of == sequence[0]) | (sink == sequence[0]) | (tallies[sink] == 0), 0, jnp.maximum(room, 0))
    shifted = jax.random.randint(jax.random.fold_in(own, 4), (number_of // 2,), 0, 1 << 20) % (room + 1)
    tallies = tallies.at[source_of].add(-shifted).at[sink].add(shifted)
    items = jnp.searchsorted(jnp.cumsum(tallies), jnp.arange(rows * top), side="right").astype(jnp.int32)
    listing = items.reshape(top, rows).T
    listing = listing[jax.random.permutation(jax.random.fold_in(own, 1), rows)]
    rotation = jax.random.randint(jax.random.fold_in(own, 2), (rows, 1), 0, top)
    return jnp.take_along_axis(listing, (jnp.arange(top)[None, :] + rotation) % top, axis=1)


def portions_of(amount, total, reach, lean, full):
    weights = [(1 << 20) // math.isqrt(standing ** lean) + 1 for standing in range(1, amount + 1)]
    largest = reach if full else min(reach, max(-(-total // amount), total * weights[0] // sum(weights)))
    least = 1 if total - largest >= amount - 1 else 0
    counts, surplus = [largest] + [least] * (amount - 1), total - largest - least * (amount - 1)
    while surplus > 0:
        free = [i for i in range(1, amount) if counts[i] < largest] or [i for i in range(1, amount) if counts[i] < reach]
        mass, remaining = sum([weights[i] for i in free]), surplus
        for i in free:
            more = min(reach - counts[i], max(1, remaining * weights[i] // mass), surplus)
            counts[i] = counts[i] + more
            surplus = surplus - more
    return np.array(counts)


def normal_values(stream_key, extent, width, limit, shards=(), kind=jnp.bfloat16):
    values = width * jax.random.normal(stream_key, extent, jnp.float32)
    if shards:
        values = values * steps_of(stream_key, extent, shards, -0.22, 0.18)
    return jnp.clip(values, -limit, limit).astype(kind)


def setup_inputs(seed: int = 0) -> dict:
    splits = jax.random.split(jax.random.key(seed), 8)
    tokens = normal_values(splits[0], (TOKENS, D), 1.0, 6.0, ((0, 32),))
    cotangent = normal_values(splits[1], (TOKENS, D), 1.0, 6.0, ((0, 32),))
    expert_ids_keys = jax.random.split(jax.random.fold_in(splits[2], 1), TOKENS // TOK_DEV)
    expert_ids_turns = jax.random.permutation(jax.random.fold_in(splits[2], 3), TOKENS // TOK_DEV)
    expert_ids = jax.vmap(lambda own, number: assign_block(jax.random.fold_in(splits[2], 2), own, number, TOK_DEV, EXPERTS, TOP, CAP, 2))(expert_ids_keys, expert_ids_turns).reshape((TOKENS, TOP))
    gate_values = jnp.clip(0.099609375 + 0.9003906 * jax.random.uniform(splits[3], (TOKENS, TOP), jnp.float32) ** steps_of(splits[3], (TOKENS, TOP), ((0, 32),), -0.2, 0.2), 0.099609375, 1.0).astype(jnp.bfloat16)
    gate_weights = normal_values(splits[4], (EXPERTS, D, F), D ** -0.5, 0.125, ((0, 4),))
    up_weights = normal_values(splits[5], (EXPERTS, D, F), D ** -0.5, 0.125, ((0, 4),))
    down_weights = normal_values(splits[6], (EXPERTS, F, D), F ** -0.5, 0.25, ((0, 4),))
    return dict(tokens=tokens, cotangent=cotangent, expert_ids=expert_ids, gate_values=gate_values, gate_weights=gate_weights, up_weights=up_weights, down_weights=down_weights)


def expert_pass(rows_x, rows_dy, rows_gates, w_gate, w_up, w_down):
    pre_gate = jnp.dot(rows_x, w_gate, preferred_element_type=jnp.float32)
    pre_up = jnp.dot(rows_x, w_up, preferred_element_type=jnp.float32)
    sigmoid_of = jax.nn.sigmoid(pre_gate)
    activated = pre_gate * sigmoid_of
    hidden = (activated * pre_up).astype(jnp.bfloat16)
    scaled = (rows_gates[:, None].astype(jnp.float32) * rows_dy.astype(jnp.float32)).astype(jnp.bfloat16)
    down_grad = lax.dot_general(hidden, scaled, (((0,), (0,)), ((), ())), preferred_element_type=jnp.float32)
    contract_cols = (((1,), (1,)), ((), ()))
    hidden_back = lax.dot_general(scaled, w_down, contract_cols, preferred_element_type=jnp.float32)
    gate_back = (hidden_back * pre_up * sigmoid_of * (1.0 + pre_gate * (1.0 - sigmoid_of))).astype(jnp.bfloat16)
    up_back = (hidden_back * activated).astype(jnp.bfloat16)
    row_grads = lax.dot_general(gate_back, w_gate, contract_cols, preferred_element_type=jnp.float32)
    row_grads = row_grads + lax.dot_general(up_back, w_up, contract_cols, preferred_element_type=jnp.float32)
    return row_grads.astype(jnp.bfloat16), down_grad


def reference(tokens, cotangent, expert_ids, gate_values, gate_weights, up_weights, down_weights):
    blocks = TOKENS // TOK_DEV
    per_block = TOK_DEV * TOP
    slot_total = TOKENS * TOP
    ids_blocks = expert_ids.reshape(blocks, per_block)
    columns = jnp.arange(EXPERTS).astype(jnp.int32)
    one_hot = (ids_blocks[:, :, None] == columns[None, None, :]).astype(jnp.int32)
    earlier = jnp.cumsum(one_hot, axis=1) - one_hot
    position = jnp.sum(one_hot * earlier, axis=2).astype(jnp.int32)
    block_index = jnp.arange(blocks).astype(jnp.int32)[:, None]
    target = ids_blocks * (blocks * CAP) + block_index * CAP + position
    slot_ids = jnp.arange(slot_total).astype(jnp.int32)
    table = jnp.full((EXPERTS * blocks * CAP,), slot_total, jnp.int32)
    table = table.at[target.reshape(-1).astype(jnp.int32)].set(slot_ids).reshape(EXPERTS, blocks * CAP)
    flat_gates = gate_values.reshape(slot_total)

    def per_expert(running, inputs):
        slot_list, w_gate, w_up, w_down = inputs
        token_rows = (slot_list // TOP).astype(jnp.int32)
        rows_x = jnp.take(tokens, token_rows, axis=0, mode="fill", fill_value=0)
        rows_dy = jnp.take(cotangent, token_rows, axis=0, mode="fill", fill_value=0)
        rows_gates = jnp.take(flat_gates, slot_list, axis=0, mode="fill", fill_value=0)
        row_grads, down_grad = expert_pass(rows_x, rows_dy, rows_gates, w_gate, w_up, w_down)
        running = running.at[token_rows].add(row_grads.astype(jnp.float32), mode="drop")
        return running, down_grad

    accumulated, down_grads = lax.scan(per_expert, jnp.zeros((TOKENS, D), jnp.float32), (table, gate_weights, up_weights, down_weights))
    return accumulated.astype(jnp.bfloat16), down_grads
```

```python
import functools

import jax
import jax.numpy as jnp
from jax import lax
from jax.experimental import pallas as pl
from jax.experimental.pallas import tpu as pltpu
from jax.sharding import PartitionSpec as P


F32 = jnp.float32
BF16 = jnp.bfloat16
LANES = 128
CONTRACT_COLS = (((1,), (1,)), ((), ()))
CONTRACT_ROWS = (((0,), (0,)), ((), ()))
VMEM_SPEC = pl.BlockSpec(memory_space=pltpu.VMEM)


def call(kernel, out_shapes, flops, args, vmem_mib, name):
    moved = sum(a.size * a.dtype.itemsize for a in args)
    moved += sum(int(jnp.dtype(o.dtype).itemsize) * o.size for o in out_shapes)
    return pl.pallas_call(
        kernel,
        out_shape=out_shapes,
        in_specs=[VMEM_SPEC] * len(args),
        out_specs=[VMEM_SPEC] * len(out_shapes),
        compiler_params=pltpu.CompilerParams(vmem_limit_bytes=vmem_mib * 1024 * 1024),
        cost_estimate=pl.CostEstimate(flops=flops, bytes_accessed=moved, transcendentals=0),
        name=name,
    )(*args)


def stacked(refs):
    if len(refs) == 1:
        return refs[0][...]
    return jnp.concatenate([r[...] for r in refs], axis=0)


def gate_column(gates):
    lane = lax.broadcasted_iota(jnp.int32, gates.shape, 1)
    mine = lane == lax.axis_index("expert")
    return jnp.sum(jnp.where(mine, gates.astype(F32), 0.0), axis=1, keepdims=True)


def hidden_kernel(count, *refs):
    rows = stacked(refs[:count])
    w_gate, w_up, hidden, gate_factor, up_factor = refs[count:]
    pre_gate = jnp.dot(rows, w_gate[...], preferred_element_type=F32)
    pre_up = jnp.dot(rows, w_up[...], preferred_element_type=F32)
    sig = jax.nn.sigmoid(pre_gate)
    act = pre_gate * sig
    hidden[...] = (act * pre_up).astype(BF16)
    gate_factor[...] = pre_up * sig * (1.0 + pre_gate * (1.0 - sig))
    up_factor[...] = act


def down_kernel(groups, count, bit, dp, *refs):
    hidden = stacked(refs[:groups])
    grads = stacked(refs[groups : groups + count])
    gates = gate_column(stacked(refs[groups + count : groups + 2 * count]))
    send, keep = refs[groups + 2 * count :]
    scaled = (gates * grads.astype(F32)).astype(BF16)
    total = lax.dot_general(hidden, scaled, CONTRACT_ROWS, preferred_element_type=F32)
    size = total.shape[0] // dp
    mine = lax.rem(lax.div(lax.axis_index("dp"), 1 << bit), 2)
    for side in range(2):

        @pl.when(mine == side)
        def _():
            for block in range(dp):
                slot = (block >> (bit + 1) << bit) | (block & ((1 << bit) - 1))
                part = total[block * size : (block + 1) * size]
                if (block >> bit) & 1 == side:
                    keep[slot] = part
                else:
                    send[slot] = part.astype(BF16)


def rows_kernel(count, chunks, *refs):
    grads = [stacked(refs[c * count : (c + 1) * count]) for c in range(chunks)]
    refs = refs[chunks * count :]
    gates = gate_column(stacked(refs[:count]))
    gate_factor, up_factor, w_gate, w_up, w_down = refs[count : count + 5]
    outs = refs[count + 5 :]
    back, at = None, 0
    for part in grads:
        scaled = (gates * part.astype(F32)).astype(BF16)
        width = part.shape[1]
        term = lax.dot_general(
            scaled, w_down[:, at : at + width], CONTRACT_COLS, preferred_element_type=F32
        )
        back = term if back is None else back + term
        at += width
    gate_back = (back * gate_factor[...]).astype(BF16)
    up_back = (back * up_factor[...]).astype(BF16)
    total = lax.dot_general(gate_back, w_gate[...], CONTRACT_COLS, preferred_element_type=F32)
    total += lax.dot_general(up_back, w_up[...], CONTRACT_COLS, preferred_element_type=F32)
    total = total.astype(BF16)
    size = total.shape[0] // count
    for i, out in enumerate(outs):
        out[...] = total[i * size : (i + 1) * size]


def swap(value, axis, bit):
    size = lax.axis_size(axis)
    return lax.ppermute(value, axis, [(i, i ^ (1 << bit)) for i in range(size)])


def spread(value, bits):
    out = [value]
    for bit in bits:
        out += [swap(v, "expert", bit) for v in out]
    return out


def halves(total, index, bit):
    inner = 1 << bit
    shape = total.shape
    view = total.reshape((shape[0] // (2 * inner), 2, inner) + shape[1:])
    out = (shape[0] // 2,) + shape[1:]
    keep = lax.dynamic_index_in_dim(view, index, 1, keepdims=False).reshape(out)
    send = lax.dynamic_index_in_dim(view, 1 - index, 1, keepdims=False).reshape(out)
    return send.astype(BF16), keep


def body(tokens, cotangent, expert_ids, gate_values, gate_weights, up_weights, down_weights):
    experts, dp = lax.axis_size("expert"), lax.axis_size("dp")
    rows, width = tokens.shape
    hidden_width = gate_weights.shape[2]
    bits = experts.bit_length() - 1
    dp_bits = dp.bit_length() - 1
    chunks = 2
    step = width // chunks
    w_gate, w_up, w_down = gate_weights[0], up_weights[0], down_weights[0]

    lane = lax.broadcasted_iota(jnp.int32, (rows, LANES), 1)
    table = jnp.zeros((rows, LANES), BF16)
    for k in range(expert_ids.shape[1]):
        table = jnp.where(lane == expert_ids[:, k : k + 1], gate_values[:, k : k + 1], table)

    top, low = bits - 1, list(range(bits - 1))
    pieces = [cotangent[:, c * step : (c + 1) * step] for c in range(chunks)]
    pieces[0] = jnp.concatenate([pieces[0], table], axis=1)
    near_tokens = spread(tokens, low)
    near_pieces = [spread(p, low) for p in pieces]
    far_tokens = spread(swap(tokens, "expert", top), low)
    far_pieces = [spread(swap(p, "expert", top), low) for p in pieces]

    count = len(near_tokens)
    group_rows = count * rows
    mat = 2 * group_rows * width * hidden_width

    def unpack(groups):
        gates = [p[:, step:] for p in groups[0]]
        return [[p[:, :step] for p in groups[0]]] + groups[1:], gates

    near_pieces, near_gates = unpack(near_pieces)
    far_pieces, far_gates = unpack(far_pieces)

    def hidden_of(blocks):
        shape = (group_rows, hidden_width)
        outs = [jax.ShapeDtypeStruct(shape, t) for t in (BF16, F32, F32)]
        return call(
            functools.partial(hidden_kernel, count), outs, 2 * mat, [*blocks, w_gate, w_up], 24, "hidden"
        )

    def rows_of(pieces, gates, factors):
        outs = [jax.ShapeDtypeStruct((rows, width), BF16)] * count
        args = [p for group in pieces for p in group] + [*gates, *factors, w_gate, w_up, w_down]
        return call(functools.partial(rows_kernel, count, chunks), outs, 3 * mat, args, 32, "rows")

    near_hidden, *near_factors = hidden_of(near_tokens)
    near_rows = rows_of(near_pieces, near_gates, near_factors)
    far_hidden, *far_factors = hidden_of(far_tokens)

    place = lax.axis_index("dp")
    block = hidden_width // dp
    down_out = []
    for c in range(chunks):
        order = list(range(dp_bits))
        if c % 2 and dp_bits > 1:
            order[0], order[1] = order[1], order[0]
        parts = near_pieces[c] + far_pieces[c]
        outs = [
            jax.ShapeDtypeStruct((dp // 2, block, step), BF16),
            jax.ShapeDtypeStruct((dp // 2, block, step), F32),
        ]
        args = [near_hidden, far_hidden, *parts, *near_gates, *far_gates]
        send, keep = call(
            functools.partial(down_kernel, 2, len(parts), order[0], dp), outs, 2 * mat // chunks, args, 24, "down"
        )
        left = [b for b in range(dp_bits)]
        for at, bit in enumerate(order):
            total = keep + swap(send, "dp", bit).astype(F32)
            left.remove(bit)
            if at + 1 < dp_bits:
                nxt = order[at + 1]
                send, keep = halves(total, (place >> nxt) & 1, left.index(nxt))
        down_out.append(total.reshape(block, step))
    down = jnp.concatenate(down_out, axis=1)

    far_rows = rows_of(far_pieces, far_gates, far_factors)

    def gathered(blocks):
        for bit in reversed(low):
            half = len(blocks) // 2
            got = [swap(b, "expert", bit) for b in blocks[half:]]
            blocks = [
                a.astype(F32) + g.astype(F32) if isinstance(g, jax.Array) else a
                for a, g in zip(blocks[:half], got)
            ]
            if half > 1:
                blocks = [b.astype(BF16) for b in blocks]
        return blocks[0]

    far_total = swap(gathered(far_rows).astype(BF16), "expert", top)
    token_grads = (gathered(near_rows) + far_total.astype(F32)).astype(BF16)
    return (token_grads, down[None])


def wide_body(tokens, cotangent, expert_ids, gate_values, gate_weights, up_weights, down_weights):
    experts_here = lax.axis_size("expert")
    tok_count, model_width = tokens.shape
    choices_per = expert_ids.shape[1]
    capacity = tok_count * choices_per * 9 // (8 * experts_here)
    slot_total = tok_count * choices_per
    flat_ids = expert_ids.reshape(slot_total)
    columns = jnp.arange(experts_here, dtype=jnp.int32)
    one_hot = (flat_ids[:, None] == columns[None, :]).astype(jnp.int32)
    earlier = jnp.cumsum(one_hot, axis=0) - one_hot
    position = jnp.sum(one_hot * earlier, axis=1)
    target = flat_ids * capacity + position
    slot_ids = jnp.arange(slot_total, dtype=jnp.int32)
    source = jnp.full((experts_here * capacity,), slot_total, jnp.int32).at[target].set(slot_ids)
    source_token = source // choices_per
    sent_rows = jnp.take(tokens, source_token, axis=0, mode="fill", fill_value=0).reshape(
        experts_here, capacity, model_width
    )
    sent_grads = jnp.take(cotangent, source_token, axis=0, mode="fill", fill_value=0).reshape(
        experts_here, capacity, model_width
    )
    sent_gates = jnp.take(
        gate_values.reshape(slot_total), source, axis=0, mode="fill", fill_value=0
    ).reshape(experts_here, capacity)
    w_gate = gate_weights[0]
    w_up = up_weights[0]
    w_down = down_weights[0]
    arrived = lax.all_to_all(sent_rows, "expert", split_axis=0, concat_axis=0, tiled=True).reshape(
        -1, model_width
    )
    pre_gate = jnp.dot(arrived, w_gate, preferred_element_type=jnp.float32)
    pre_up = jnp.dot(arrived, w_up, preferred_element_type=jnp.float32)
    sigmoid_of = jax.nn.sigmoid(pre_gate)
    activated = pre_gate * sigmoid_of
    hidden = (activated * pre_up).astype(jnp.bfloat16)
    arrived_grads, arrived_gates = (
        lax.all_to_all(sent_grads, "expert", split_axis=0, concat_axis=0, tiled=True),
        lax.all_to_all(sent_gates, "expert", split_axis=0, concat_axis=0, tiled=True),
    )
    scaled = (
        arrived_gates.reshape(-1)[:, None].astype(jnp.float32)
        * arrived_grads.reshape(-1, model_width).astype(jnp.float32)
    ).astype(jnp.bfloat16)
    hidden_back = lax.dot_general(scaled, w_down, CONTRACT_COLS, preferred_element_type=jnp.float32)
    gate_back = (hidden_back * pre_up * sigmoid_of * (1.0 + pre_gate * (1.0 - sigmoid_of))).astype(
        jnp.bfloat16
    )
    up_back = (hidden_back * activated).astype(jnp.bfloat16)
    row_grads = lax.dot_general(gate_back, w_gate, CONTRACT_COLS, preferred_element_type=jnp.float32)
    row_grads = (
        row_grads
        + lax.dot_general(up_back, w_up, CONTRACT_COLS, preferred_element_type=jnp.float32)
    ).astype(jnp.bfloat16)
    returned = lax.all_to_all(
        row_grads.reshape(experts_here, capacity, model_width),
        "expert",
        split_axis=0,
        concat_axis=0,
        tiled=True,
    )
    picked = jnp.take(returned.reshape(-1, model_width), target, axis=0).astype(jnp.float32)
    token_grads = jnp.sum(picked.reshape(tok_count, choices_per, model_width), axis=1).astype(
        jnp.bfloat16
    )
    down_part = lax.psum_scatter(
        lax.dot_general(
            hidden, scaled, (((0,), (0,)), ((), ())), preferred_element_type=jnp.float32
        ),
        "dp",
        scatter_dimension=0,
        tiled=True,
    )
    return (token_grads, down_part[None])


def power_of_two(n):
    return n > 1 and n & (n - 1) == 0


def solution(mesh):
    experts, dp = mesh.shape["expert"], mesh.shape["dp"]
    dense = experts * experts <= 16 and power_of_two(experts) and power_of_two(dp)
    return jax.shard_map(
        body if dense else wide_body,
        mesh=mesh,
        in_specs=(
            P(("dp", "expert"), None),
            P(("dp", "expert"), None),
            P(("dp", "expert"), None),
            P(("dp", "expert"), None),
            P("expert", None, None),
            P("expert", None, None),
            P("expert", None, None),
        ),
        out_specs=(P(("dp", "expert"), None), P("expert", "dp", None)),
        check_vma=False,
    )
```

```python
import functools

import jax
import jax.numpy as jnp
from jax import lax
from jax.experimental import pallas as pl
from jax.experimental.pallas import tpu as pltpu
from jax.sharding import PartitionSpec as P


F32 = jnp.float32
BF16 = jnp.bfloat16
LANES = 128
CHUNK_PARTS = (5, 4, 4, 3)
FIRST_BIT = (0, 1, 0, 0)
CONTRACT_COLS = (((1,), (1,)), ((), ()))
CONTRACT_ROWS = (((0,), (0,)), ((), ()))
VMEM_SPEC = pl.BlockSpec(memory_space=pltpu.VMEM)
HBM_SPEC = pl.BlockSpec(memory_space=pltpu.HBM)


def call(kernel, out_shapes, args, flops=0, vmem_mib=16, in_hbm=False, scratch=()):
    moved = sum(a.size * a.dtype.itemsize for a in args)
    moved += sum(jnp.dtype(o.dtype).itemsize * o.size for o in out_shapes)
    return pl.pallas_call(
        kernel,
        out_shape=out_shapes,
        in_specs=[HBM_SPEC if in_hbm else VMEM_SPEC] * len(args),
        out_specs=[VMEM_SPEC] * len(out_shapes),
        scratch_shapes=list(scratch),
        compiler_params=pltpu.CompilerParams(vmem_limit_bytes=vmem_mib * 1024 * 1024),
        cost_estimate=pl.CostEstimate(flops=flops, bytes_accessed=moved, transcendentals=0),
    )(*args)


def stacked(parts):
    return parts[0] if len(parts) == 1 else jnp.concatenate(parts, axis=0)


def gate_column(tagged, width):
    gates = stacked([t[:, width:] for t in tagged]).astype(F32)
    mine = lax.broadcasted_iota(jnp.int32, gates.shape, 1) == lax.axis_index("expert")
    return jnp.sum(jnp.where(mine, gates, 0.0), axis=1, keepdims=True)


def bit_of(axis, bit):
    return lax.rem(lax.div(lax.axis_index(axis), 1 << bit), 2)


def copy_all(sources, targets, sems):
    copies = [pltpu.make_async_copy(s, t, sems.at[i]) for i, (s, t) in enumerate(zip(sources, targets))]
    for c in copies:
        c.start()
    for c in copies:
        c.wait()


def load_kernel(count, *refs):
    copy_all(refs[:count], refs[count : 2 * count], refs[-1])


def prep_kernel(edges, choices, *refs):
    pieces = refs[3:-4]
    grads, ids, gates, sems = refs[-4:]
    copy_all(refs[:3], (grads, ids, gates), sems)
    experts = lax.broadcasted_iota(jnp.int32, (LANES, grads.shape[0]), 0)
    table = jnp.zeros(experts.shape, F32)
    values = gates[...].astype(F32)
    for k in range(choices):
        table = jnp.where(experts == ids[k : k + 1, :], values[k : k + 1, :], table)
    for at, piece in enumerate(pieces):
        low, high = edges[at], edges[at + 1]
        piece[:, : high - low] = grads[:, low:high]
    pieces[0][:, edges[1] :] = table.T.astype(BF16)


def hidden_kernel(count, *refs):
    rows = stacked([r[...] for r in refs[:count]])
    w_gate, w_up, hidden, gate_factor, up_factor = refs[count:]
    pre_gate = jnp.dot(rows, w_gate[...], preferred_element_type=F32)
    pre_up = jnp.dot(rows, w_up[...], preferred_element_type=F32)
    sig = jax.nn.sigmoid(pre_gate)
    act = pre_gate * sig
    hidden[...] = (act * pre_up).astype(BF16)
    gate_factor[...] = pre_up * sig * (1.0 + pre_gate * (1.0 - sig))
    up_factor[...] = act


def split_blocks(total, bit, mine, send, keep):
    blocks = send.shape[0] * 2
    size = total.shape[0] // blocks
    for side in range(2):

        @pl.when(mine == side)
        def _():
            for block in range(blocks):
                slot = (block >> (bit + 1) << bit) | (block & ((1 << bit) - 1))
                part = total[block * size : (block + 1) * size]
                if (block >> bit) & 1 == side:
                    keep[slot] = part
                else:
                    send[slot] = part.astype(BF16)


def down_kernel(count, width, bit, separate, *refs):
    hidden = stacked([r[...] for r in refs[:2]])
    tagged = refs[2 : 2 + count]
    parts = refs[2 + count : 2 + 2 * count] if separate else tagged
    send, keep = refs[-2:]
    wide = send.shape[2]
    gates = gate_column(tagged, width)
    grads = stacked([p[:, :wide] for p in parts])
    scaled = (gates * grads.astype(F32)).astype(BF16)
    total = lax.dot_general(hidden, scaled, CONTRACT_ROWS, preferred_element_type=F32)
    split_blocks(total, bit, bit_of("dp", bit), send, keep)


def merge_kernel(bit, place, keep_in, arrived, send, keep):
    blocks, size, wide = keep_in.shape
    total = keep_in[...] + arrived[...].astype(F32)
    split_blocks(total.reshape(blocks * size, wide), place, bit_of("dp", bit), send, keep)


def finish_kernel(edges, *refs):
    out = refs[-1]
    for at in range(len(edges) - 1):
        out[:, edges[at] : edges[at + 1]] = refs[2 * at][0] + refs[2 * at + 1][0].astype(F32)


def rows_kernel(count, edges, *refs):
    chunks = len(edges) - 1
    gates = gate_column(refs[:count], edges[1])
    gate_factor, up_factor, w_gate, w_up, w_down = refs[chunks * count : chunks * count + 5]
    outs = refs[chunks * count + 5 :]
    back = None
    for c in range(chunks):
        low, high = edges[c], edges[c + 1]
        part = stacked([r[:, : high - low] for r in refs[c * count : (c + 1) * count]])
        scaled = (gates * part.astype(F32)).astype(BF16)
        term = lax.dot_general(scaled, w_down[:, low:high], CONTRACT_COLS, preferred_element_type=F32)
        back = term if back is None else back + term
    gate_back = (back * gate_factor[...]).astype(BF16)
    up_back = (back * up_factor[...]).astype(BF16)
    total = lax.dot_general(gate_back, w_gate[...], CONTRACT_COLS, preferred_element_type=F32)
    total += lax.dot_general(up_back, w_up[...], CONTRACT_COLS, preferred_element_type=F32)
    total = total.astype(BF16)
    size = total.shape[0] // count
    for i, out in enumerate(outs):
        out[...] = total[i * size : (i + 1) * size]


def sum_kernel(*refs):
    total = refs[0][...].astype(F32)
    for r in refs[1:-1]:
        total = total + r[...].astype(F32)
    refs[-1][...] = total.astype(BF16)


def swap(value, axis, bit):
    size = lax.axis_size(axis)
    return lax.ppermute(value, axis, [(i, i ^ (1 << bit)) for i in range(size)])


def spread(value, bits):
    out = [value]
    for bit in bits:
        out += [swap(v, "expert", bit) for v in out]
    return out


def column_edges(width):
    parts = sum(CHUNK_PARTS)
    if width % (LANES * parts):
        return (0, width)
    edges = [0]
    for p in CHUNK_PARTS:
        edges.append(edges[-1] + p * (width // parts))
    return tuple(edges)


def narrow_body(tokens, cotangent, expert_ids, gate_values, gate_weights, up_weights, down_weights):
    experts, dp = lax.axis_size("expert"), lax.axis_size("dp")
    rows, width = tokens.shape
    hidden_width = gate_weights.shape[2]
    choices = expert_ids.shape[1]
    dp_bits = dp.bit_length() - 1
    top = experts.bit_length() - 2
    low = list(range(top))
    edges = column_edges(width)
    chunks = len(edges) - 1
    widths = [b - a for a, b in zip(edges, edges[1:])]
    struct = jax.ShapeDtypeStruct

    far_first = swap(tokens, "expert", top)
    near_tokens = spread(tokens, low)
    pieces = call(
        functools.partial(prep_kernel, edges, choices),
        [struct((rows, w + (LANES if c == 0 else 0)), BF16) for c, w in enumerate(widths)],
        [cotangent, expert_ids.T, gate_values.T],
        vmem_mib=56,
        in_hbm=True,
        scratch=[
            pltpu.VMEM((rows, width), BF16),
            pltpu.VMEM((choices, rows), jnp.int32),
            pltpu.VMEM((choices, rows), BF16),
            pltpu.SemaphoreType.DMA((3,)),
        ],
    )
    kept = [gate_weights[0], up_weights[0], down_weights[0], tokens]
    w_gate, w_up, w_down, own_tokens = call(
        functools.partial(load_kernel, len(kept)),
        [struct(a.shape, a.dtype) for a in kept],
        kept,
        vmem_mib=46,
        in_hbm=True,
        scratch=[pltpu.SemaphoreType.DMA((len(kept),))],
    )
    far_pieces = [swap(p, "expert", top) for p in pieces]
    near_pieces = [spread(p, low) for p in pieces]
    far_tokens = spread(far_first, low)
    far_pieces = [spread(p, low) for p in far_pieces]
    count = len(near_tokens)
    group_rows = count * rows
    mat = 2 * group_rows * width * hidden_width

    def hidden_of(blocks):
        shape = (group_rows, hidden_width)
        return call(
            functools.partial(hidden_kernel, count),
            [struct(shape, t) for t in (BF16, F32, F32)],
            [*blocks, w_gate, w_up],
            2 * mat,
        )

    def rows_of(groups, factors):
        args = [p for group in groups for p in group] + [*factors, w_gate, w_up, w_down]
        return call(
            functools.partial(rows_kernel, count, edges),
            [struct((rows, width), BF16)] * count,
            args,
            3 * mat,
        )

    def gathered(blocks):
        for bit in reversed(low):
            half = len(blocks) // 2
            got = [swap(b, "expert", bit) for b in blocks[half:]]
            if half == 1:
                return [blocks[0], got[0]]
            blocks = [
                call(sum_kernel, [struct((rows, width), BF16)], [a, g])[0]
                for a, g in zip(blocks, got)
            ]
        return blocks

    near_hidden, *near_factors = hidden_of([own_tokens, *near_tokens[1:]])
    near_rows = rows_of(near_pieces, near_factors)
    near_terms = gathered(near_rows)
    far_hidden, *far_factors = hidden_of(far_tokens)

    block = hidden_width // dp
    down_terms = []
    for c in range(chunks):
        order = list(range(dp_bits))
        first = FIRST_BIT[c] if dp_bits > 1 else 0
        order[0], order[first] = order[first], order[0]
        tagged = near_pieces[0] + far_pieces[0]
        parts = near_pieces[c] + far_pieces[c] if c else []
        send, keep = call(
            functools.partial(down_kernel, len(tagged), widths[0], order[0], c > 0),
            [struct((dp // 2, block, widths[c]), t) for t in (BF16, F32)],
            [near_hidden, far_hidden, *tagged, *parts],
            2 * mat * widths[c] // width,
        )
        left = list(range(dp_bits))
        for at, bit in enumerate(order):
            arrived = swap(send, "dp", bit)
            left.remove(bit)
            if at + 1 < dp_bits:
                nxt = order[at + 1]
                half = struct((keep.shape[0] // 2, block, widths[c]), F32)
                send, keep = call(
                    functools.partial(merge_kernel, nxt, left.index(nxt)),
                    [struct(half.shape, BF16), half],
                    [keep, arrived],
                )
        down_terms += [keep, arrived]
    down = call(
        functools.partial(finish_kernel, edges), [struct((block, width), F32)], down_terms
    )[0]

    far_rows = rows_of(far_pieces, far_factors)
    far_terms = gathered(far_rows)
    if len(far_terms) > 1:
        far_terms = call(sum_kernel, [struct((rows, width), BF16)], far_terms)
    far_total = swap(far_terms[0], "expert", top)
    token_grads = call(sum_kernel, [struct((rows, width), BF16)], [*near_terms, far_total])[0]
    return (token_grads, down[None])


def body(*args):
    return narrow_body(*args)


def wide_body(tokens, cotangent, expert_ids, gate_values, gate_weights, up_weights, down_weights):
    experts_here = lax.axis_size("expert")
    tok_count, model_width = tokens.shape
    choices_per = expert_ids.shape[1]
    capacity = tok_count * choices_per * 9 // (8 * experts_here)
    slot_total = tok_count * choices_per
    flat_ids = expert_ids.reshape(slot_total)
    columns = jnp.arange(experts_here, dtype=jnp.int32)
    one_hot = (flat_ids[:, None] == columns[None, :]).astype(jnp.int32)
    earlier = jnp.cumsum(one_hot, axis=0) - one_hot
    position = jnp.sum(one_hot * earlier, axis=1)
    target = flat_ids * capacity + position
    slot_ids = jnp.arange(slot_total, dtype=jnp.int32)
    source = jnp.full((experts_here * capacity,), slot_total, jnp.int32).at[target].set(slot_ids)
    source_token = source // choices_per
    sent_rows = jnp.take(tokens, source_token, axis=0, mode="fill", fill_value=0).reshape(
        experts_here, capacity, model_width
    )
    sent_grads = jnp.take(cotangent, source_token, axis=0, mode="fill", fill_value=0).reshape(
        experts_here, capacity, model_width
    )
    sent_gates = jnp.take(
        gate_values.reshape(slot_total), source, axis=0, mode="fill", fill_value=0
    ).reshape(experts_here, capacity)
    w_gate = gate_weights[0]
    w_up = up_weights[0]
    w_down = down_weights[0]
    arrived = lax.all_to_all(sent_rows, "expert", split_axis=0, concat_axis=0, tiled=True).reshape(
        -1, model_width
    )
    pre_gate = jnp.dot(arrived, w_gate, preferred_element_type=jnp.float32)
    pre_up = jnp.dot(arrived, w_up, preferred_element_type=jnp.float32)
    sigmoid_of = jax.nn.sigmoid(pre_gate)
    activated = pre_gate * sigmoid_of
    hidden = (activated * pre_up).astype(jnp.bfloat16)
    arrived_grads, arrived_gates = (
        lax.all_to_all(sent_grads, "expert", split_axis=0, concat_axis=0, tiled=True),
        lax.all_to_all(sent_gates, "expert", split_axis=0, concat_axis=0, tiled=True),
    )
    scaled = (
        arrived_gates.reshape(-1)[:, None].astype(jnp.float32)
        * arrived_grads.reshape(-1, model_width).astype(jnp.float32)
    ).astype(jnp.bfloat16)
    hidden_back = lax.dot_general(scaled, w_down, CONTRACT_COLS, preferred_element_type=jnp.float32)
    gate_back = (hidden_back * pre_up * sigmoid_of * (1.0 + pre_gate * (1.0 - sigmoid_of))).astype(
        jnp.bfloat16
    )
    up_back = (hidden_back * activated).astype(jnp.bfloat16)
    row_grads = lax.dot_general(gate_back, w_gate, CONTRACT_COLS, preferred_element_type=jnp.float32)
    row_grads = (
        row_grads
        + lax.dot_general(up_back, w_up, CONTRACT_COLS, preferred_element_type=jnp.float32)
    ).astype(jnp.bfloat16)
    returned = lax.all_to_all(
        row_grads.reshape(experts_here, capacity, model_width),
        "expert",
        split_axis=0,
        concat_axis=0,
        tiled=True,
    )
    picked = jnp.take(returned.reshape(-1, model_width), target, axis=0).astype(jnp.float32)
    token_grads = jnp.sum(picked.reshape(tok_count, choices_per, model_width), axis=1).astype(
        jnp.bfloat16
    )
    down_part = lax.psum_scatter(
        lax.dot_general(
            hidden, scaled, (((0,), (0,)), ((), ())), preferred_element_type=jnp.float32
        ),
        "dp",
        scatter_dimension=0,
        tiled=True,
    )
    return (token_grads, down_part[None])


def power_of_two(n):
    return n > 1 and n & (n - 1) == 0


def solution(mesh):
    experts, dp = mesh.shape["expert"], mesh.shape["dp"]
    narrow = power_of_two(experts) and power_of_two(dp) and experts <= 4
    return jax.shard_map(
        body if narrow else wide_body,
        mesh=mesh,
        in_specs=(
            P(("dp", "expert"), None),
            P(("dp", "expert"), None),
            P(("dp", "expert"), None),
            P(("dp", "expert"), None),
            P("expert", None, None),
            P("expert", None, None),
            P("expert", None, None),
        ),
        out_specs=(P(("dp", "expert"), None), P("expert", "dp", None)),
        check_vma=False,
    )
```

```python
import functools

import jax
import jax.numpy as jnp
from jax import lax
from jax.experimental import pallas as pl
from jax.experimental.pallas import tpu as pltpu
from jax.sharding import PartitionSpec as P


F32 = jnp.float32
BF16 = jnp.bfloat16
LANES = 128
CHUNK_PARTS = (5, 4, 4, 3)
CHUNK_ORDERS = ((0, 1, 2), (1, 0, 2), (0, 1, 2), (0, 1, 2))
CONTRACT_COLS = (((1,), (1,)), ((), ()))
CONTRACT_ROWS = (((0,), (0,)), ((), ()))
VMEM_SPEC = pl.BlockSpec(memory_space=pltpu.VMEM)
HBM_SPEC = pl.BlockSpec(memory_space=pltpu.HBM)


def call(kernel, out_shapes, args, flops=0, vmem_mib=16, in_hbm=False, scratch=()):
    moved = sum(a.size * a.dtype.itemsize for a in args)
    moved += sum(jnp.dtype(o.dtype).itemsize * o.size for o in out_shapes)
    return pl.pallas_call(
        kernel,
        out_shape=out_shapes,
        in_specs=[HBM_SPEC if in_hbm else VMEM_SPEC] * len(args),
        out_specs=[VMEM_SPEC] * len(out_shapes),
        scratch_shapes=list(scratch),
        compiler_params=pltpu.CompilerParams(vmem_limit_bytes=vmem_mib * 1024 * 1024),
        cost_estimate=pl.CostEstimate(flops=flops, bytes_accessed=moved, transcendentals=0),
    )(*args)


def stacked(parts):
    return parts[0] if len(parts) == 1 else jnp.concatenate(parts, axis=0)


def gate_column(tagged, width):
    gates = stacked([t[:, width:] for t in tagged]).astype(F32)
    mine = lax.broadcasted_iota(jnp.int32, gates.shape, 1) == lax.axis_index("expert")
    return jnp.sum(jnp.where(mine, gates, 0.0), axis=1, keepdims=True)


def bit_of(axis, bit):
    return lax.rem(lax.div(lax.axis_index(axis), 1 << bit), 2)


def copy_all(sources, targets, sems):
    copies = [pltpu.make_async_copy(s, t, sems.at[i]) for i, (s, t) in enumerate(zip(sources, targets))]
    for c in copies:
        c.start()
    for c in copies:
        c.wait()


def load_kernel(count, *refs):
    copy_all(refs[:count], refs[count : 2 * count], refs[-1])


def prep_kernel(edges, choices, *refs):
    pieces = refs[3:-4]
    grads, ids, gates, sems = refs[-4:]
    copy_all(refs[:3], (grads, ids, gates), sems)
    experts = lax.broadcasted_iota(jnp.int32, (LANES, grads.shape[0]), 0)
    table = jnp.zeros(experts.shape, F32)
    values = gates[...].astype(F32)
    for k in range(choices):
        table = jnp.where(experts == ids[k : k + 1, :], values[k : k + 1, :], table)
    for at, piece in enumerate(pieces):
        low, high = edges[at], edges[at + 1]
        piece[:, : high - low] = grads[:, low:high]
    pieces[0][:, edges[1] :] = table.T.astype(BF16)


def hidden_kernel(count, *refs):
    rows = stacked([r[...] for r in refs[:count]])
    w_gate, w_up, hidden, gate_factor, up_factor = refs[count:]
    pre_gate = jnp.dot(rows, w_gate[...], preferred_element_type=F32)
    pre_up = jnp.dot(rows, w_up[...], preferred_element_type=F32)
    sig = jax.nn.sigmoid(pre_gate)
    act = pre_gate * sig
    hidden[...] = (act * pre_up).astype(BF16)
    gate_factor[...] = pre_up * sig * (1.0 + pre_gate * (1.0 - sig))
    up_factor[...] = act


def split_blocks(total, bit, mine, send, keep):
    blocks = send.shape[0] * 2
    size = total.shape[0] // blocks
    for side in range(2):

        @pl.when(mine == side)
        def _():
            for block in range(blocks):
                slot = (block >> (bit + 1) << bit) | (block & ((1 << bit) - 1))
                part = total[block * size : (block + 1) * size]
                if (block >> bit) & 1 == side:
                    keep[slot] = part
                else:
                    send[slot] = part.astype(BF16)


def down_kernel(count, width, bit, separate, *refs):
    hidden = stacked([r[...] for r in refs[:2]])
    tagged = refs[2 : 2 + count]
    parts = refs[2 + count : 2 + 2 * count] if separate else tagged
    send, keep = refs[-2:]
    wide = send.shape[2]
    gates = gate_column(tagged, width)
    grads = stacked([p[:, :wide] for p in parts])
    scaled = (gates * grads.astype(F32)).astype(BF16)
    total = lax.dot_general(hidden, scaled, CONTRACT_ROWS, preferred_element_type=F32)
    split_blocks(total, bit, bit_of("dp", bit), send, keep)


def merge_kernel(bit, place, keep_in, arrived, send, keep):
    blocks, size, wide = keep_in.shape
    total = keep_in[...] + arrived[...].astype(F32)
    split_blocks(total.reshape(blocks * size, wide), place, bit_of("dp", bit), send, keep)


def finish_kernel(edges, *refs):
    out = refs[-1]
    for at in range(len(edges) - 1):
        out[:, edges[at] : edges[at + 1]] = refs[2 * at][0] + refs[2 * at + 1][0].astype(F32)


def rows_kernel(count, edges, *refs):
    chunks = len(edges) - 1
    gates = gate_column(refs[:count], edges[1])
    gate_factor, up_factor, w_gate, w_up, w_down = refs[chunks * count : chunks * count + 5]
    outs = refs[chunks * count + 5 :]
    back = None
    for c in range(chunks):
        low, high = edges[c], edges[c + 1]
        part = stacked([r[:, : high - low] for r in refs[c * count : (c + 1) * count]])
        scaled = (gates * part.astype(F32)).astype(BF16)
        term = lax.dot_general(scaled, w_down[:, low:high], CONTRACT_COLS, preferred_element_type=F32)
        back = term if back is None else back + term
    gate_back = (back * gate_factor[...]).astype(BF16)
    up_back = (back * up_factor[...]).astype(BF16)
    total = lax.dot_general(gate_back, w_gate[...], CONTRACT_COLS, preferred_element_type=F32)
    total += lax.dot_general(up_back, w_up[...], CONTRACT_COLS, preferred_element_type=F32)
    total = total.astype(BF16)
    size = total.shape[0] // count
    for i, out in enumerate(outs):
        out[...] = total[i * size : (i + 1) * size]


def sum_kernel(*refs):
    total = refs[0][...].astype(F32)
    for r in refs[1:-1]:
        total = total + r[...].astype(F32)
    refs[-1][...] = total.astype(BF16)


def swap(value, axis, bit):
    size = lax.axis_size(axis)
    return lax.ppermute(value, axis, [(i, i ^ (1 << bit)) for i in range(size)])


def spread(value, bits):
    out = [value]
    for bit in bits:
        out += [swap(v, "expert", bit) for v in out]
    return out


def column_edges(width):
    parts = sum(CHUNK_PARTS)
    if width % (LANES * parts):
        return (0, width)
    edges = [0]
    for p in CHUNK_PARTS:
        edges.append(edges[-1] + p * (width // parts))
    return tuple(edges)


def narrow_body(tokens, cotangent, expert_ids, gate_values, gate_weights, up_weights, down_weights):
    experts, dp = lax.axis_size("expert"), lax.axis_size("dp")
    rows, width = tokens.shape
    hidden_width = gate_weights.shape[2]
    choices = expert_ids.shape[1]
    dp_bits = dp.bit_length() - 1
    top = experts.bit_length() - 2
    low = list(range(top))
    edges = column_edges(width)
    chunks = len(edges) - 1
    widths = [b - a for a, b in zip(edges, edges[1:])]
    struct = jax.ShapeDtypeStruct

    far_first = swap(tokens, "expert", top)
    near_tokens = spread(tokens, low)
    pieces = call(
        functools.partial(prep_kernel, edges, choices),
        [struct((rows, w + (LANES if c == 0 else 0)), BF16) for c, w in enumerate(widths)],
        [cotangent, expert_ids.T, gate_values.T],
        vmem_mib=56,
        in_hbm=True,
        scratch=[
            pltpu.VMEM((rows, width), BF16),
            pltpu.VMEM((choices, rows), jnp.int32),
            pltpu.VMEM((choices, rows), BF16),
            pltpu.SemaphoreType.DMA((3,)),
        ],
    )
    kept = [gate_weights[0], up_weights[0], down_weights[0], tokens]
    w_gate, w_up, w_down, own_tokens = call(
        functools.partial(load_kernel, len(kept)),
        [struct(a.shape, a.dtype) for a in kept],
        kept,
        vmem_mib=46,
        in_hbm=True,
        scratch=[pltpu.SemaphoreType.DMA((len(kept),))],
    )
    far_pieces = [swap(p, "expert", top) for p in pieces]
    near_pieces = [spread(p, low) for p in pieces]
    far_tokens = spread(far_first, low)
    far_pieces = [spread(p, low) for p in far_pieces]
    count = len(near_tokens)
    group_rows = count * rows
    mat = 2 * group_rows * width * hidden_width

    def hidden_of(blocks):
        shape = (group_rows, hidden_width)
        return call(
            functools.partial(hidden_kernel, count),
            [struct(shape, t) for t in (BF16, F32, F32)],
            [*blocks, w_gate, w_up],
            2 * mat,
        )

    def rows_of(groups, factors):
        args = [p for group in groups for p in group] + [*factors, w_gate, w_up, w_down]
        return call(
            functools.partial(rows_kernel, count, edges),
            [struct((rows, width), BF16)] * count,
            args,
            3 * mat,
        )

    def gathered(blocks):
        for bit in reversed(low):
            half = len(blocks) // 2
            got = [swap(b, "expert", bit) for b in blocks[half:]]
            if half == 1:
                return [blocks[0], got[0]]
            blocks = [
                call(sum_kernel, [struct((rows, width), BF16)], [a, g])[0]
                for a, g in zip(blocks, got)
            ]
        return blocks

    near_hidden, *near_factors = hidden_of([own_tokens, *near_tokens[1:]])
    near_rows = rows_of(near_pieces, near_factors)
    near_terms = gathered(near_rows)
    far_hidden, *far_factors = hidden_of(far_tokens)

    block = hidden_width // dp
    down_terms = []
    for c in range(chunks):
        order = CHUNK_ORDERS[c] if dp_bits == len(CHUNK_ORDERS[c]) else tuple(range(dp_bits))
        tagged = near_pieces[0] + far_pieces[0]
        parts = near_pieces[c] + far_pieces[c] if c else []
        send, keep = call(
            functools.partial(down_kernel, len(tagged), widths[0], order[0], c > 0),
            [struct((dp // 2, block, widths[c]), t) for t in (BF16, F32)],
            [near_hidden, far_hidden, *tagged, *parts],
            2 * mat * widths[c] // width,
        )
        left = list(range(dp_bits))
        for at, bit in enumerate(order):
            arrived = swap(send, "dp", bit)
            left.remove(bit)
            if at + 1 < dp_bits:
                nxt = order[at + 1]
                half = struct((keep.shape[0] // 2, block, widths[c]), F32)
                send, keep = call(
                    functools.partial(merge_kernel, nxt, left.index(nxt)),
                    [struct(half.shape, BF16), half],
                    [keep, arrived],
                )
        down_terms += [keep, arrived]
    down = call(
        functools.partial(finish_kernel, edges), [struct((block, width), F32)], down_terms
    )[0]

    far_rows = rows_of(far_pieces, far_factors)
    far_terms = gathered(far_rows)
    if len(far_terms) > 1:
        far_terms = call(sum_kernel, [struct((rows, width), BF16)], far_terms)
    far_total = swap(far_terms[0], "expert", top)
    token_grads = call(sum_kernel, [struct((rows, width), BF16)], [*near_terms, far_total])[0]
    return (token_grads, down[None])


def body(*args):
    return narrow_body(*args)


def wide_body(tokens, cotangent, expert_ids, gate_values, gate_weights, up_weights, down_weights):
    experts_here = lax.axis_size("expert")
    tok_count, model_width = tokens.shape
    choices_per = expert_ids.shape[1]
    capacity = tok_count * choices_per * 9 // (8 * experts_here)
    slot_total = tok_count * choices_per
    flat_ids = expert_ids.reshape(slot_total)
    columns = jnp.arange(experts_here, dtype=jnp.int32)
    one_hot = (flat_ids[:, None] == columns[None, :]).astype(jnp.int32)
    earlier = jnp.cumsum(one_hot, axis=0) - one_hot
    position = jnp.sum(one_hot * earlier, axis=1)
    target = flat_ids * capacity + position
    slot_ids = jnp.arange(slot_total, dtype=jnp.int32)
    source = jnp.full((experts_here * capacity,), slot_total, jnp.int32).at[target].set(slot_ids)
    source_token = source // choices_per
    sent_rows = jnp.take(tokens, source_token, axis=0, mode="fill", fill_value=0).reshape(
        experts_here, capacity, model_width
    )
    sent_grads = jnp.take(cotangent, source_token, axis=0, mode="fill", fill_value=0).reshape(
        experts_here, capacity, model_width
    )
    sent_gates = jnp.take(
        gate_values.reshape(slot_total), source, axis=0, mode="fill", fill_value=0
    ).reshape(experts_here, capacity)
    w_gate = gate_weights[0]
    w_up = up_weights[0]
    w_down = down_weights[0]
    arrived = lax.all_to_all(sent_rows, "expert", split_axis=0, concat_axis=0, tiled=True).reshape(
        -1, model_width
    )
    pre_gate = jnp.dot(arrived, w_gate, preferred_element_type=jnp.float32)
    pre_up = jnp.dot(arrived, w_up, preferred_element_type=jnp.float32)
    sigmoid_of = jax.nn.sigmoid(pre_gate)
    activated = pre_gate * sigmoid_of
    hidden = (activated * pre_up).astype(jnp.bfloat16)
    arrived_grads, arrived_gates = (
        lax.all_to_all(sent_grads, "expert", split_axis=0, concat_axis=0, tiled=True),
        lax.all_to_all(sent_gates, "expert", split_axis=0, concat_axis=0, tiled=True),
    )
    scaled = (
        arrived_gates.reshape(-1)[:, None].astype(jnp.float32)
        * arrived_grads.reshape(-1, model_width).astype(jnp.float32)
    ).astype(jnp.bfloat16)
    hidden_back = lax.dot_general(scaled, w_down, CONTRACT_COLS, preferred_element_type=jnp.float32)
    gate_back = (hidden_back * pre_up * sigmoid_of * (1.0 + pre_gate * (1.0 - sigmoid_of))).astype(
        jnp.bfloat16
    )
    up_back = (hidden_back * activated).astype(jnp.bfloat16)
    row_grads = lax.dot_general(gate_back, w_gate, CONTRACT_COLS, preferred_element_type=jnp.float32)
    row_grads = (
        row_grads
        + lax.dot_general(up_back, w_up, CONTRACT_COLS, preferred_element_type=jnp.float32)
    ).astype(jnp.bfloat16)
    returned = lax.all_to_all(
        row_grads.reshape(experts_here, capacity, model_width),
        "expert",
        split_axis=0,
        concat_axis=0,
        tiled=True,
    )
    picked = jnp.take(returned.reshape(-1, model_width), target, axis=0).astype(jnp.float32)
    token_grads = jnp.sum(picked.reshape(tok_count, choices_per, model_width), axis=1).astype(
        jnp.bfloat16
    )
    down_part = lax.psum_scatter(
        lax.dot_general(
            hidden, scaled, (((0,), (0,)), ((), ())), preferred_element_type=jnp.float32
        ),
        "dp",
        scatter_dimension=0,
        tiled=True,
    )
    return (token_grads, down_part[None])


def power_of_two(n):
    return n > 1 and n & (n - 1) == 0


def solution(mesh):
    experts, dp = mesh.shape["expert"], mesh.shape["dp"]
    narrow = power_of_two(experts) and power_of_two(dp) and experts <= 4
    return jax.shard_map(
        body if narrow else wide_body,
        mesh=mesh,
        in_specs=(
            P(("dp", "expert"), None),
            P(("dp", "expert"), None),
            P(("dp", "expert"), None),
            P(("dp", "expert"), None),
            P("expert", None, None),
            P("expert", None, None),
            P("expert", None, None),
        ),
        out_specs=(P(("dp", "expert"), None), P("expert", "dp", None)),
        check_vma=False,
    )
```
